32 devices in a mesh: heads: 1, seq: 32 (over z, y, x, core).
Axes of the slice: x: 2, y: 2, z: 4, core: 2. Of those that a mesh axis runs over, the one named last changes fastest.
Arguments:
- queries: bfloat16 [65536, 2, 512], P('seq', 'heads'), may hold values from -6 to 6
- key_rows: bfloat16 [65536, 2, 512], P('seq', 'heads'), may hold values from -6 to 6
- value_rows: bfloat16 [65536, 2, 512], P('seq', 'heads'), may hold values from -6 to 6
- step_rates: bfloat16 [2, 65536], P('heads', 'seq'), may hold values from 0.25 to 4
- live_counts: int32 [32], replicated, may hold values from 256 to 2048, as said below
- group_scales: float32 [2], P('heads'), may hold values from 0.4 to 1.8
- w_first: float32 [2, 512, 512], P('heads', 'seq'), may hold values from -0.8838835 to 0.8838835
- w_third: float32 [2, 512, 512], P('heads', 'seq'), may hold values from -0.8838835 to 0.8838835
- w_second: float32 [2, 512, 512], P('heads', 'seq'), may hold values from -0.8838835 to 0.8838835
Outputs:
- fast_out: bfloat16 [65536, 2, 512], P('seq', 'heads')
The draws below stay inside these ranges and needn't reach their ends.
Inputs may be any that keep to these rules, and one draw needn't show every extreme that they name: `live_counts`: live token count of each clip shard; every draw has one shard of 2048 live tokens.
All inputs are finite; a program needn't handle non-finite values.
Results may differ from the reference program's by a relative error of at most 0.012.
The reference program's roundings to bfloat16 on the way count: a program that leaves them out, or rounds other values in their place, can miss the bound.
Values may be sent and summed in bfloat16 or wider, within the bound.
A program may use at most 128 MiB of HBM per device.

```python
import math
import jax
import jax.numpy as jnp
from jax import lax

WIDTH = 512
GROUPS = 2
CAP = 2048
TOKENS = 65536
N_SEQ = 32


def fast_weight(key, salt):
    base_key, row_key = jax.random.split(jax.random.fold_in(key, salt))
    base = jnp.clip(jax.random.normal(base_key, (GROUPS, WIDTH, WIDTH), jnp.float32), -4.0, 4.0)
    row_scale = jnp.exp(jax.random.uniform(row_key, (GROUPS, WIDTH, 1), jnp.float32, math.log(0.5), math.log(5.0)))
    return base * row_scale / math.sqrt(WIDTH)


def draw_w_first(key, part):
    return fast_weight(key, 11)


def draw_w_third(key, part):
    return fast_weight(key, 13)


def draw_w_second(key, part):
    return fast_weight(key, 17)


def draw_group_scales(key, part):
    ramp = jnp.arange(GROUPS, dtype=jnp.float32) / max(GROUPS - 1, 1)
    noise = jax.random.uniform(jax.random.fold_in(key, 23), (GROUPS,), jnp.float32, 0.85, 1.15)
    return 0.5 * jnp.exp(ramp * math.log(3.0)) * noise


def draw_live_counts(key, part):
    base_key, order_key, heavy_key = jax.random.split(jax.random.fold_in(key, 29), 3)
    light = jax.random.randint(base_key, (N_SEQ,), CAP // 8, CAP // 2 + 1)
    heavy = jax.random.randint(heavy_key, (N_SEQ,), CAP // 2, CAP + 1)
    order = jax.random.permutation(order_key, N_SEQ)
    counts = jnp.where(order < 3, heavy, light)
    return jnp.where(order == 0, CAP, counts).astype(jnp.int32)


def levels(own_key, extent, pieces, low, top_value):
    level, own = 1.0, jax.random.fold_in(own_key, 6)
    for dim, parts in pieces:
        heights = jnp.exp(jax.random.uniform(jax.random.fold_in(own, dim), (parts,), jnp.float32, low / len(pieces), top_value / len(pieces)))
        level = level * jnp.repeat(heights, extent[dim] // parts).reshape([-1 if axis == dim else 1 for axis in range(len(extent))])
    return level


def normal_values(own_key, dims, spread, bound, shards=(), kind=jnp.bfloat16):
    entries = spread * jax.random.normal(own_key, dims, jnp.float32)
    if shards:
        entries = entries * levels(own_key, dims, shards, -0.22, 0.18)
    return jnp.clip(entries, -bound, bound).astype(kind)


def setup_inputs(seed: int = 0) -> dict:
    arg_keys = jax.random.split(jax.random.key(seed), 10)
    return {
        "queries": normal_values(arg_keys[0], (TOKENS, GROUPS, WIDTH), 1.0, 6.0, ((0, 32),)),
        "key_rows": normal_values(arg_keys[1], (TOKENS, GROUPS, WIDTH), 1.0, 6.0, ((0, 32),)),
        "value_rows": normal_values(arg_keys[2], (TOKENS, GROUPS, WIDTH), 1.0, 6.0, ((0, 32),)),
        "step_rates": jnp.clip(jnp.exp(math.log(4.0) - 2.7725887 * jax.random.uniform(arg_keys[3], (GROUPS, TOKENS), jnp.float32) ** levels(arg_keys[3], (GROUPS, TOKENS), ((1, 32),), -0.2, 0.2)), 0.25, 4.0).astype(jnp.bfloat16),
        "live_counts": draw_live_counts(jax.random.fold_in(arg_keys[9], 71), 0),
        "group_scales": draw_group_scales(jax.random.fold_in(arg_keys[9], 71), 0),
        "w_first": draw_w_first(jax.random.fold_in(arg_keys[9], 71), 0),
        "w_third": draw_w_third(jax.random.fold_in(arg_keys[9], 71), 0),
        "w_second": draw_w_second(jax.random.fold_in(arg_keys[9], 71), 0),
    }


EPS = 1e-06

def row_normalize(start_w, update):
    norm_old = jnp.sqrt(lax.optimization_barrier(jnp.mean(start_w * start_w, axis=-1, keepdims=True)) + EPS)
    norm_new = jnp.sqrt(lax.optimization_barrier(jnp.mean(update * update, axis=-1, keepdims=True)) + EPS)
    return update * (norm_old / norm_new)

def reference(queries, key_rows, value_rows, step_rates, live_counts, group_scales, w_first, w_third, w_second):
    total = queries.shape[0]
    position = jnp.arange(total, dtype=jnp.int32)
    owner_count = live_counts[position // CAP]
    live = position % CAP < owner_count
    live_f = live.astype(jnp.float32)
    live_b = live.astype(jnp.bfloat16)[:, None]
    root_total = math.sqrt(total)
    outputs = []
    for group in range(GROUPS):
        k_part = key_rows[:, group]
        v_part = value_rows[:, group]
        q_part = queries[:, group]
        eta = step_rates[group].astype(jnp.float32) * live_f / root_total
        b_one = w_first[group].astype(jnp.bfloat16)
        b_three = w_third[group].astype(jnp.bfloat16)
        b_two = w_second[group].astype(jnp.bfloat16)
        h_one = jnp.dot(k_part, b_one, preferred_element_type=jnp.float32)
        h_three = jnp.dot(k_part, b_three, preferred_element_type=jnp.float32)
        gate = jax.nn.silu(h_one)
        act = (gate * h_three).astype(jnp.bfloat16)
        err = (eta[:, None] * v_part.astype(jnp.float32)).astype(jnp.bfloat16)
        back = jnp.dot(err, b_two.T, preferred_element_type=jnp.float32)
        sig = jax.nn.sigmoid(h_one)
        d_one = (back * h_three * (sig * (1.0 + h_one * (1.0 - sig)))).astype(jnp.bfloat16)
        d_three = (back * gate).astype(jnp.bfloat16)
        p_one = jnp.dot(k_part.T, d_one, preferred_element_type=jnp.float32)
        p_three = jnp.dot(k_part.T, d_three, preferred_element_type=jnp.float32)
        p_two = jnp.dot(act.T, err, preferred_element_type=jnp.float32)
        c_one = row_normalize(w_first[group], w_first[group] + p_one).astype(jnp.bfloat16)
        c_three = row_normalize(w_third[group], w_third[group] + p_three).astype(jnp.bfloat16)
        c_two = row_normalize(w_second[group], w_second[group] + p_two).astype(jnp.bfloat16)
        q_one = jnp.dot(q_part, c_one, preferred_element_type=jnp.float32)
        q_three = jnp.dot(q_part, c_three, preferred_element_type=jnp.float32)
        a_query = (jax.nn.silu(q_one) * q_three).astype(jnp.bfloat16)
        o_part = jnp.dot(a_query, c_two, preferred_element_type=jnp.float32).astype(jnp.bfloat16) * live_b
        outputs.append(o_part.astype(jnp.float32) * group_scales[group])
    total_sq = jnp.zeros((total,), jnp.float32)
    for group in range(GROUPS):
        total_sq = total_sq + lax.optimization_barrier(jnp.sum(outputs[group] * outputs[group], axis=-1))
    factor = lax.rsqrt(total_sq / (GROUPS * WIDTH) + EPS)[:, None]
    return jnp.stack([(wide * factor).astype(jnp.bfloat16) for wide in outputs], axis=1)
```

```python
import functools

import jax
import jax.numpy as jnp
from jax import lax
from jax.experimental import pallas as pl
from jax.experimental.pallas import tpu as pltpu
from jax.sharding import PartitionSpec as P

EPS = 1e-06
MESH = pl.DeviceIdType.MESH
LANES = 128
VMEM_LIMIT = 60 * 1024 * 1024


def ring_maps(chips):
    if chips != 16:
        return (lambda chip: chip), (lambda pos: pos)

    def pos_of(chip):
        z, y, x = chip // 4, (chip // 2) % 2, chip % 2
        p = y * 3 + x - 2 * x * y
        row = 3 - z
        odd = row % 2
        m = (1 - odd) * (p - 1) + odd * (3 - p)
        snake = 4 + 3 * row + m
        off = (p + 3) // 4
        return (1 - off) * z + off * snake

    def chip_of(pos):
        on = pos // 4
        on = (on + 3) // 4
        k = (pos + 12) % 16
        row = k // 3
        m = k % 3
        odd = row % 2
        p = (1 - odd) * (m + 1) + odd * (3 - m)
        z = (1 - on) * pos + on * (3 - row)
        p = on * p
        y = p // 2
        x = (y + p) % 2
        return z * 4 + y * 2 + x

    return pos_of, chip_of


class Ring:
    def __init__(self, n):
        self.chips = n // 2
        self.pos_of, self.chip_of = ring_maps(self.chips)
        me = lax.axis_index("seq")
        self.core = me % 2
        self.partner = me + 1 - 2 * self.core
        self.chip = me // 2
        self.pos = self.pos_of(self.chip)
        self.right_steps = self.chips // 2
        self.left_steps = self.chips - 1 - self.right_steps
        self.right = self.index(1)
        self.left = self.index(-1)

    def index(self, offset):
        return self.chip_at(offset) * 2 + self.core

    def chip_at(self, offset):
        return self.chip_of((self.pos + offset + self.chips) % self.chips)

    def barrier(self):
        sem = pltpu.get_barrier_semaphore()
        for peer in (self.left, self.right, self.partner):
            pl.semaphore_signal(sem, inc=1, device_id={"seq": peer}, device_id_type=MESH)
        pl.semaphore_wait(sem, 3)


def remote(src, dst, send_sem, recv_sem, peer):
    return pltpu.make_async_remote_copy(
        src_ref=src, dst_ref=dst, send_sem=send_sem, recv_sem=recv_sem,
        device_id={"seq": peer}, device_id_type=MESH,
    )


def gather_ring(ring, own, out, sems):
    groups = own.shape[0]
    rs, rr, ls, lr, ps, pr = sems
    me = lax.axis_index("seq")
    for g in range(groups):
        out[g, :, me] = own[g]

    def slot(g, idx):
        return out.at[g, :, idx]

    def right_copy(s, g, src):
        dst = slot(g, ring.index(-s))
        return remote(dst if src is None else src, dst, rs.at[s, g], rr.at[s, g], ring.right)

    def left_copy(s, g, src):
        dst = slot(g, ring.index(s))
        return remote(dst if src is None else src, dst, ls.at[s, g], lr.at[s, g], ring.left)

    def partner_copy(k, g, offset, src):
        dst = slot(g, ring.index(offset))
        return remote(dst if src is None else src, dst, ps.at[k, g], pr.at[k, g], ring.partner)

    for g in range(groups):
        right_copy(0, g, own.at[g]).start()
        left_copy(0, g, own.at[g]).start()
        partner_copy(0, g, 0, own.at[g]).start()

    def step(s, carry):
        for g in range(groups):
            right_copy(s - 1, g, None).wait_recv()

            @pl.when(s < ring.right_steps)
            def _():
                right_copy(s, g, None).start()

            partner_copy(s, g, -s, None).start()

            @pl.when(s <= ring.left_steps)
            def _():
                left_copy(s - 1, g, None).wait_recv()

                @pl.when(s < ring.left_steps)
                def _():
                    left_copy(s, g, None).start()

                partner_copy(ring.right_steps + s, g, s, None).start()

        return carry

    lax.fori_loop(1, ring.right_steps + 1, step, 0)

    def drain(s, carry):
        for g in range(groups):
            right_copy(s, g, None).wait_send()

            @pl.when(s < ring.left_steps)
            def _():
                left_copy(s, g, None).wait_send()

        return carry

    lax.fori_loop(0, ring.right_steps, drain, 0)

    def drain_partner(k, carry):
        for g in range(groups):
            copy = partner_copy(k, g, 0, None)
            copy.wait_send()
            copy.wait_recv()
        return carry

    lax.fori_loop(0, ring.chips, drain_partner, 0)


def gather_sems(ring_chips, groups):
    right = ring_chips // 2
    left = max(ring_chips - 1 - right, 1)
    dma = pltpu.SemaphoreType.DMA
    return [dma((right, groups)), dma((right, groups)), dma((left, groups)), dma((left, groups)),
            dma((ring_chips, groups)), dma((ring_chips, groups))]


def gather_kernel(n, own_ref, out_ref, *sems):
    ring = Ring(n)
    ring.barrier()
    gather_ring(ring, own_ref, out_ref, sems)


def gather_rows(n, own):
    groups, kinds, rows, feats = own.shape
    return pl.pallas_call(
        functools.partial(gather_kernel, n),
        out_shape=jax.ShapeDtypeStruct((groups, kinds, n, rows, feats), own.dtype),
        in_specs=[pl.BlockSpec(memory_space=pltpu.VMEM)],
        out_specs=pl.BlockSpec(memory_space=pltpu.VMEM),
        scratch_shapes=gather_sems(n // 2, groups),
        compiler_params=pltpu.CompilerParams(
            collective_id=0, has_side_effects=True, vmem_limit_bytes=VMEM_LIMIT
        ),
        name="gather_start",
    )(own)


def reduce_kernel(n, part_ref, w_ref, out_ref, pair, pair_in, buf_r, buf_l, in_r, in_l, fresh,
                  xs, xr, rs, rr, ls, lr, *gsems):
    ring = Ring(n)
    groups = w_ref.shape[0]
    ring.barrier()
    exchange = [
        remote(part_ref.at[g, :, :, 1 - ring.core], pair_in.at[g], xs.at[g], xr.at[g], ring.partner)
        for g in range(groups)
    ]
    for copy in exchange:
        copy.start()

    def right_copy(s, g):
        return remote(buf_r.at[s, g], in_r.at[s, g], rs.at[s, g], rr.at[s, g], ring.right)

    def left_copy(s, g):
        return remote(buf_l.at[s, g], in_l.at[s, g], ls.at[s, g], lr.at[s, g], ring.left)

    def both(g, chip):
        return (part_ref[g, :, chip, ring.core].astype(jnp.float32)
                + pair_in[g, :, chip].astype(jnp.float32))

    for g in range(groups):
        exchange[g].wait_recv()
        buf_r[0, g] = both(g, ring.chip_at(ring.right_steps)).astype(buf_r.dtype)
        right_copy(0, g).start()
        buf_l[0, g] = both(g, ring.chip_at(-ring.left_steps)).astype(buf_l.dtype)
        left_copy(0, g).start()

    def step(s, carry):
        for g in range(groups):
            own = both(g, ring.chip_at(ring.right_steps - s))
            right_copy(s - 1, g).wait_recv()
            buf_r[s, g] = (own + in_r[s - 1, g].astype(jnp.float32)).astype(buf_r.dtype)
            right_copy(s, g).start()

            @pl.when(s < ring.left_steps)
            def _():
                own_l = both(g, ring.chip_at(s - ring.left_steps))
                left_copy(s - 1, g).wait_recv()
                buf_l[s, g] = (own_l + in_l[s - 1, g].astype(jnp.float32)).astype(buf_l.dtype)
                left_copy(s, g).start()

        return carry

    lax.fori_loop(1, ring.right_steps, step, 0)
    for g in range(groups):
        left_copy(ring.left_steps - 1, g).wait_recv()
        right_copy(ring.right_steps - 1, g).wait_recv()
        term = (both(g, ring.chip) + in_l[ring.left_steps - 1, g].astype(jnp.float32)
                + in_r[ring.right_steps - 1, g].astype(jnp.float32))
        start_w = w_ref[g]
        update = start_w + term
        norm_old = jnp.sqrt(jnp.mean(start_w * start_w, axis=-1, keepdims=True) + EPS)
        norm_new = jnp.sqrt(jnp.mean(update * update, axis=-1, keepdims=True) + EPS)
        fresh[g] = (update * (norm_old / norm_new)).astype(fresh.dtype)

    gather_ring(ring, fresh, out_ref, gsems)
    for g in range(groups):
        exchange[g].wait_send()

    def drain(s, carry):
        for g in range(groups):
            right_copy(s, g).wait_send()

            @pl.when(s < ring.left_steps)
            def _():
                left_copy(s, g).wait_send()

        return carry

    lax.fori_loop(0, ring.right_steps, drain, 0)


def reduce_rows(n, part, w_own):
    groups, kinds, rows, feats = w_own.shape
    chips = n // 2
    right = chips // 2
    left = chips - 1 - right
    piece = (groups, kinds, rows, feats)
    dma = pltpu.SemaphoreType.DMA
    bf = jnp.bfloat16
    return pl.pallas_call(
        functools.partial(reduce_kernel, n),
        out_shape=jax.ShapeDtypeStruct((groups, kinds, n, rows, feats), bf),
        in_specs=[pl.BlockSpec(memory_space=pltpu.VMEM)] * 2,
        out_specs=pl.BlockSpec(memory_space=pltpu.VMEM),
        scratch_shapes=[
            pltpu.VMEM((8, LANES), bf),
            pltpu.VMEM((groups, kinds, chips, rows, feats), bf),
            pltpu.VMEM((right,) + piece, bf),
            pltpu.VMEM((left,) + piece, bf),
            pltpu.VMEM((right,) + piece, bf),
            pltpu.VMEM((left,) + piece, bf),
            pltpu.VMEM(piece, bf),
            dma((groups,)), dma((groups,)),
            dma((right, groups)), dma((right, groups)),
            dma((left, groups)), dma((left, groups)),
        ] + gather_sems(chips, groups),
        compiler_params=pltpu.CompilerParams(
            collective_id=1, has_side_effects=True, vmem_limit_bytes=VMEM_LIMIT
        ),
        name="reduce_gather",
    )(part, w_own)


def to_view(rows):
    tokens, groups, feats = rows.shape
    cuts = feats // LANES
    return rows.reshape(tokens, groups, cuts, LANES).transpose(0, 2, 1, 3).reshape(-1, LANES)


def from_view(view, shape):
    tokens, groups, feats = shape
    cuts = feats // LANES
    return view.reshape(tokens, cuts, groups, LANES).transpose(0, 2, 1, 3).reshape(shape)


def pick(scr, g, groups, cuts, tile):
    step = groups * cuts
    cols = [scr[pl.ds(c * groups + g, tile, stride=step), :] for c in range(cuts)]
    return jnp.concatenate(cols, axis=-1).astype(jnp.bfloat16)


def dot(a, b, dims):
    return lax.dot_general(a, b, (dims, ((), ())), preferred_element_type=jnp.float32)


def sigmoid(x):
    return 0.5 * jnp.tanh(0.5 * x) + 0.5


def terms_kernel(groups, cuts, tile, k_ref, v_ref, eta_ref, b_ref, out_ref, k_scr, v_scr, acc):
    i = pl.program_id(0)

    @pl.when(i == 0)
    def _():
        acc[...] = jnp.zeros_like(acc)

    k_scr[...] = k_ref[...].astype(jnp.float32)
    v_scr[...] = v_ref[...].astype(jnp.float32)
    for g in range(groups):
        k = pick(k_scr, g, groups, cuts, tile)
        v = pick(v_scr, g, groups, cuts, tile)
        err = (eta_ref[:, g:g + 1] * v.astype(jnp.float32)).astype(jnp.bfloat16)
        h_one = dot(k, b_ref[g, 0], ((1,), (0,)))
        h_three = dot(k, b_ref[g, 1], ((1,), (0,)))
        back = dot(err, b_ref[g, 2], ((1,), (1,)))
        sig = sigmoid(h_one)
        gate = h_one * sig
        act = (gate * h_three).astype(jnp.bfloat16)
        d_one = (back * h_three * (sig * (1.0 + h_one * (1.0 - sig)))).astype(jnp.bfloat16)
        d_three = (back * gate).astype(jnp.bfloat16)
        acc[g, 0] += dot(k, d_one, ((0,), (0,)))
        acc[g, 1] += dot(k, d_three, ((0,), (0,)))
        acc[g, 2] += dot(act, err, ((0,), (0,)))

    @pl.when(i == pl.num_programs(0) - 1)
    def _():
        out_ref[...] = acc[...].astype(out_ref.dtype)


def local_terms(k_view, v_view, eta_rows, halves):
    groups, kinds, width, feats = halves.shape
    cuts = feats // LANES
    tokens = eta_rows.shape[0]
    tile = min(512, tokens)
    rows = tile * groups * cuts
    whole = pl.BlockSpec(memory_space=pltpu.VMEM)
    return pl.pallas_call(
        functools.partial(terms_kernel, groups, cuts, tile),
        grid=(tokens // tile,),
        out_shape=jax.ShapeDtypeStruct(halves.shape, jnp.bfloat16),
        in_specs=[
            pl.BlockSpec((rows, LANES), lambda i: (i, 0)),
            pl.BlockSpec((rows, LANES), lambda i: (i, 0)),
            pl.BlockSpec((tile, groups), lambda i: (i, 0)),
            whole,
        ],
        out_specs=whole,
        scratch_shapes=[
            pltpu.VMEM((rows, LANES), jnp.float32),
            pltpu.VMEM((rows, LANES), jnp.float32),
            pltpu.VMEM(halves.shape, jnp.float32),
        ],
        compiler_params=pltpu.CompilerParams(vmem_limit_bytes=VMEM_LIMIT),
        name="local_terms",
    )(k_view, v_view, eta_rows, halves)


def apply_kernel(groups, cuts, tile, denom, count_ref, scale_ref, q_ref, c_ref, out_ref, q_scr, o_scr):
    i = pl.program_id(0)
    step = groups * cuts
    position = i * tile + lax.broadcasted_iota(jnp.int32, (tile, 1), 0)
    live = (position < count_ref[0]).astype(jnp.float32)
    q_scr[...] = q_ref[...].astype(jnp.float32)
    pieces = []
    total_sq = jnp.zeros((tile, 1), jnp.float32)
    for g in range(groups):
        q = pick(q_scr, g, groups, cuts, tile)
        q_one = dot(q, c_ref[g, 0], ((1,), (0,)))
        q_three = dot(q, c_ref[g, 1], ((1,), (0,)))
        a_query = (q_one * sigmoid(q_one) * q_three).astype(jnp.bfloat16)
        o = dot(a_query, c_ref[g, 2], ((1,), (0,))).astype(jnp.bfloat16)
        o = o.astype(jnp.float32) * live
        if denom is not None:
            o = o * scale_ref[g]
            total_sq = total_sq + jnp.sum(o * o, axis=-1, keepdims=True)
        pieces.append(o)
    if denom is not None:
        factor = lax.rsqrt(total_sq / denom + EPS)
        pieces = [o * factor for o in pieces]
    for g in range(groups):
        for c in range(cuts):
            o_scr[pl.ds(c * groups + g, tile, stride=step), :] = pieces[g][:, c * LANES:(c + 1) * LANES]
    out_ref[...] = o_scr[...].astype(out_ref.dtype)


def apply_rows(q_view, count, scales, fresh, tokens, denom):
    groups, kinds, width, feats = fresh.shape
    cuts = feats // LANES
    tile = min(512, tokens)
    rows = tile * groups * cuts
    smem = pl.BlockSpec(memory_space=pltpu.SMEM)
    return pl.pallas_call(
        functools.partial(apply_kernel, groups, cuts, tile, denom),
        grid=(tokens // tile,),
        out_shape=jax.ShapeDtypeStruct(q_view.shape, jnp.bfloat16),
        in_specs=[
            smem,
            smem,
            pl.BlockSpec((rows, LANES), lambda i: (i, 0)),
            pl.BlockSpec(memory_space=pltpu.VMEM),
        ],
        out_specs=pl.BlockSpec((rows, LANES), lambda i: (i, 0)),
        scratch_shapes=[
            pltpu.VMEM((rows, LANES), jnp.float32),
            pltpu.VMEM((rows, LANES), jnp.float32),
        ],
        compiler_params=pltpu.CompilerParams(vmem_limit_bytes=VMEM_LIMIT),
        name="apply_rows",
    )(count, scales, q_view, fresh)


def shards(
    queries, key_rows, value_rows, step_rates, live_counts, group_scales, w_first, w_third, w_second
):
    cap_rows, groups, feat_width = queries.shape
    seq_size = lax.axis_size("seq")
    heads = lax.axis_size("heads")
    root_total = jnp.sqrt(jnp.float32(cap_rows * seq_size))
    own_count = lax.dynamic_slice(live_counts, (lax.axis_index("seq"),), (1,))
    live_mask = jnp.arange(cap_rows, dtype=jnp.int32) < own_count[0]
    eta_rows = (
        step_rates.T.astype(jnp.float32) * live_mask.astype(jnp.float32)[:, None] / root_total
    )
    w_own = jnp.stack([w_first, w_third, w_second], axis=1)
    full = (groups, 3, feat_width, feat_width)
    chips = seq_size // 2
    own_rows = w_own.shape[2]
    halves = gather_rows(seq_size, w_own.astype(jnp.bfloat16)).reshape(full)
    part = local_terms(to_view(key_rows), to_view(value_rows), eta_rows, halves)
    part = part.reshape(groups, 3, chips, 2, own_rows, feat_width)
    fresh = reduce_rows(seq_size, part, w_own).reshape(full)
    denom = groups * feat_width * heads
    view = apply_rows(
        to_view(queries), own_count, group_scales, fresh, cap_rows, denom if heads == 1 else None
    )
    fast = from_view(view, queries.shape)
    if heads == 1:
        return fast
    wide = fast.astype(jnp.float32) * group_scales[None, :, None]
    total_sq = lax.psum(jnp.sum(wide * wide, axis=(1, 2)), "heads")
    factor = lax.rsqrt(total_sq / denom + EPS)[:, None, None]
    return (wide * factor).astype(jnp.bfloat16)


def solution(mesh):
    in_specs = (
        P("seq", "heads", None),
        P("seq", "heads", None),
        P("seq", "heads", None),
        P("heads", "seq"),
        P(),
        P("heads"),
        P("heads", "seq", None),
        P("heads", "seq", None),
        P("heads", "seq", None),
    )
    out_specs = P("seq", "heads", None)
    return jax.shard_map(shards, mesh=mesh, in_specs=in_specs, out_specs=out_specs, check_vma=False)
```

```python
import functools

import jax
import jax.numpy as jnp
from jax import lax
from jax.experimental import pallas as pl
from jax.experimental.pallas import tpu as pltpu
from jax.sharding import PartitionSpec as P

EPS = 1e-06
MESH = pl.DeviceIdType.MESH
LANES = 128
VMEM_LIMIT = 60 * 1024 * 1024


def ring_maps(chips):
    if chips != 16:
        return (lambda chip: chip), (lambda pos: pos)

    def pos_of(chip):
        z, y, x = chip // 4, (chip // 2) % 2, chip % 2
        p = y * 3 + x - 2 * x * y
        row = 3 - z
        odd = row % 2
        m = (1 - odd) * (p - 1) + odd * (3 - p)
        snake = 4 + 3 * row + m
        off = (p + 3) // 4
        return (1 - off) * z + off * snake

    def chip_of(pos):
        on = pos // 4
        on = (on + 3) // 4
        k = (pos + 12) % 16
        row = k // 3
        m = k % 3
        odd = row % 2
        p = (1 - odd) * (m + 1) + odd * (3 - m)
        z = (1 - on) * pos + on * (3 - row)
        p = on * p
        y = p // 2
        x = (y + p) % 2
        return z * 4 + y * 2 + x

    return pos_of, chip_of


class Ring:
    def __init__(self, n):
        self.chips = n // 2
        self.pos_of, self.chip_of = ring_maps(self.chips)
        me = lax.axis_index("seq")
        self.core = me % 2
        self.partner = me + 1 - 2 * self.core
        self.chip = me // 2
        self.pos = self.pos_of(self.chip)
        self.right_steps = self.chips // 2
        self.left_steps = self.chips - 1 - self.right_steps
        self.right = self.index(1)
        self.left = self.index(-1)

    def index(self, offset):
        return self.chip_at(offset) * 2 + self.core

    def chip_at(self, offset):
        return self.chip_of((self.pos + offset + self.chips) % self.chips)

    def barrier(self):
        sem = pltpu.get_barrier_semaphore()
        for peer in (self.left, self.right, self.partner):
            pl.semaphore_signal(sem, inc=1, device_id={"seq": peer}, device_id_type=MESH)
        pl.semaphore_wait(sem, 3)


def remote(src, dst, send_sem, recv_sem, peer):
    return pltpu.make_async_remote_copy(
        src_ref=src, dst_ref=dst, send_sem=send_sem, recv_sem=recv_sem,
        device_id={"seq": peer}, device_id_type=MESH,
    )


def gather_ring(ring, own, out, sems):
    groups = own.shape[0]
    rs, rr, ls, lr, ps, pr = sems
    me = lax.axis_index("seq")
    for g in range(groups):
        out[g, :, me] = own[g]

    def slot(g, idx):
        return out.at[g, :, idx]

    def right_copy(s, g, src):
        dst = slot(g, ring.index(-s))
        return remote(dst if src is None else src, dst, rs.at[s, g], rr.at[s, g], ring.right)

    def left_copy(s, g, src):
        dst = slot(g, ring.index(s))
        return remote(dst if src is None else src, dst, ls.at[s, g], lr.at[s, g], ring.left)

    def partner_copy(k, g, offset, src):
        dst = slot(g, ring.index(offset))
        return remote(dst if src is None else src, dst, ps.at[k, g], pr.at[k, g], ring.partner)

    for g in range(groups):
        right_copy(0, g, own.at[g]).start()
        left_copy(0, g, own.at[g]).start()
        partner_copy(0, g, 0, own.at[g]).start()

    def step(s, carry):
        for g in range(groups):
            right_copy(s - 1, g, None).wait_recv()

            @pl.when(s < ring.right_steps)
            def _():
                right_copy(s, g, None).start()

            partner_copy(s, g, -s, None).start()

            @pl.when(s <= ring.left_steps)
            def _():
                left_copy(s - 1, g, None).wait_recv()

                @pl.when(s < ring.left_steps)
                def _():
                    left_copy(s, g, None).start()

                partner_copy(ring.right_steps + s, g, s, None).start()

        return carry

    lax.fori_loop(1, ring.right_steps + 1, step, 0)

    def drain(s, carry):
        for g in range(groups):
            right_copy(s, g, None).wait_send()

            @pl.when(s < ring.left_steps)
            def _():
                left_copy(s, g, None).wait_send()

        return carry

    lax.fori_loop(0, ring.right_steps, drain, 0)

    def drain_partner(k, carry):
        for g in range(groups):
            copy = partner_copy(k, g, 0, None)
            copy.wait_send()
            copy.wait_recv()
        return carry

    lax.fori_loop(0, ring.chips, drain_partner, 0)


def gather_sems(ring_chips, groups):
    right = ring_chips // 2
    left = max(ring_chips - 1 - right, 1)
    dma = pltpu.SemaphoreType.DMA
    return [dma((right, groups)), dma((right, groups)), dma((left, groups)), dma((left, groups)),
            dma((ring_chips, groups)), dma((ring_chips, groups))]


def gather_kernel(n, own_ref, out_ref, *sems):
    ring = Ring(n)
    ring.barrier()
    gather_ring(ring, own_ref, out_ref, sems)


def gather_rows(n, own):
    groups, kinds, rows, feats = own.shape
    return pl.pallas_call(
        functools.partial(gather_kernel, n),
        out_shape=jax.ShapeDtypeStruct((groups, kinds, n, rows, feats), own.dtype),
        in_specs=[pl.BlockSpec(memory_space=pltpu.VMEM)],
        out_specs=pl.BlockSpec(memory_space=pltpu.VMEM),
        scratch_shapes=gather_sems(n // 2, groups),
        compiler_params=pltpu.CompilerParams(
            collective_id=0, has_side_effects=True, vmem_limit_bytes=VMEM_LIMIT
        ),
        name="gather_start",
    )(own)


def reduce_kernel(n, part_ref, w_ref, out_ref, pair_in, buf_r, buf_l, in_r, in_l, fresh,
                  xs, xr, rs, rr, ls, lr, *gsems):
    ring = Ring(n)
    groups = w_ref.shape[0]
    ring.barrier()
    exchange = [
        remote(part_ref.at[g, :, :, 1 - ring.core], pair_in.at[g], xs.at[g], xr.at[g], ring.partner)
        for g in range(groups)
    ]
    for copy in exchange:
        copy.start()

    def right_copy(s, g):
        return remote(buf_r.at[s, g], in_r.at[s, g], rs.at[s, g], rr.at[s, g], ring.right)

    def left_copy(s, g):
        return remote(buf_l.at[s, g], in_l.at[s, g], ls.at[s, g], lr.at[s, g], ring.left)

    def both(g, chip):
        return (part_ref[g, :, chip, ring.core].astype(jnp.float32)
                + pair_in[g, :, chip].astype(jnp.float32))

    for g in range(groups):
        exchange[g].wait_recv()
        buf_r[0, g] = both(g, ring.chip_at(ring.right_steps)).astype(buf_r.dtype)
        right_copy(0, g).start()
        buf_l[0, g] = both(g, ring.chip_at(-ring.left_steps)).astype(buf_l.dtype)
        left_copy(0, g).start()

    def step(s, carry):
        for g in range(groups):
            own = both(g, ring.chip_at(ring.right_steps - s))
            right_copy(s - 1, g).wait_recv()
            buf_r[s, g] = (own + in_r[s - 1, g].astype(jnp.float32)).astype(buf_r.dtype)
            right_copy(s, g).start()

            @pl.when(s < ring.left_steps)
            def _():
                own_l = both(g, ring.chip_at(s - ring.left_steps))
                left_copy(s - 1, g).wait_recv()
                buf_l[s, g] = (own_l + in_l[s - 1, g].astype(jnp.float32)).astype(buf_l.dtype)
                left_copy(s, g).start()

        return carry

    lax.fori_loop(1, ring.right_steps, step, 0)
    for g in range(groups):
        left_copy(ring.left_steps - 1, g).wait_recv()
        right_copy(ring.right_steps - 1, g).wait_recv()
        term = (both(g, ring.chip) + in_l[ring.left_steps - 1, g].astype(jnp.float32)
                + in_r[ring.right_steps - 1, g].astype(jnp.float32))
        start_w = w_ref[g]
        update = start_w + term
        norm_old = jnp.sqrt(jnp.mean(start_w * start_w, axis=-1, keepdims=True) + EPS)
        norm_new = jnp.sqrt(jnp.mean(update * update, axis=-1, keepdims=True) + EPS)
        fresh[g] = (update * (norm_old / norm_new)).astype(fresh.dtype)

    gather_ring(ring, fresh, out_ref, gsems)
    for g in range(groups):
        exchange[g].wait_send()

    def drain(s, carry):
        for g in range(groups):
            right_copy(s, g).wait_send()

            @pl.when(s < ring.left_steps)
            def _():
                left_copy(s, g).wait_send()

        return carry

    lax.fori_loop(0, ring.right_steps, drain, 0)


def reduce_rows(n, part, w_own):
    groups, kinds, rows, feats = w_own.shape
    chips = n // 2
    right = chips // 2
    left = chips - 1 - right
    piece = (groups, kinds, rows, feats)
    dma = pltpu.SemaphoreType.DMA
    bf = jnp.bfloat16
    return pl.pallas_call(
        functools.partial(reduce_kernel, n),
        out_shape=jax.ShapeDtypeStruct((groups, kinds, n, rows, feats), bf),
        in_specs=[pl.BlockSpec(memory_space=pltpu.VMEM)] * 2,
        out_specs=pl.BlockSpec(memory_space=pltpu.VMEM),
        scratch_shapes=[
            pltpu.VMEM((groups, kinds, chips, rows, feats), bf),
            pltpu.VMEM((right,) + piece, bf),
            pltpu.VMEM((left,) + piece, bf),
            pltpu.VMEM((right,) + piece, bf),
            pltpu.VMEM((left,) + piece, bf),
            pltpu.VMEM(piece, bf),
            dma((groups,)), dma((groups,)),
            dma((right, groups)), dma((right, groups)),
            dma((left, groups)), dma((left, groups)),
        ] + gather_sems(chips, groups),
        compiler_params=pltpu.CompilerParams(
            collective_id=1, has_side_effects=True, vmem_limit_bytes=VMEM_LIMIT
        ),
        name="reduce_gather",
    )(part, w_own)


def to_view(rows):
    tokens, groups, feats = rows.shape
    cuts = feats // LANES
    return rows.reshape(tokens, groups, cuts, LANES).transpose(0, 2, 1, 3).reshape(-1, LANES)


def from_view(view, shape):
    tokens, groups, feats = shape
    cuts = feats // LANES
    return view.reshape(tokens, cuts, groups, LANES).transpose(0, 2, 1, 3).reshape(shape)


def pick(scr, g, groups, cuts, tile):
    step = groups * cuts
    cols = [scr[pl.ds(c * groups + g, tile, stride=step), :] for c in range(cuts)]
    return jnp.concatenate(cols, axis=-1).astype(jnp.bfloat16)


def dot(a, b, dims):
    return lax.dot_general(a, b, (dims, ((), ())), preferred_element_type=jnp.float32)


def sigmoid(x):
    return 0.5 * jnp.tanh(0.5 * x) + 0.5


def terms_kernel(groups, cuts, tile, k_ref, v_ref, eta_ref, b_ref, out_ref, k_scr, v_scr, acc):
    i = pl.program_id(0)

    @pl.when(i == 0)
    def _():
        acc[...] = jnp.zeros_like(acc)

    k_scr[...] = k_ref[...].astype(jnp.float32)
    v_scr[...] = v_ref[...].astype(jnp.float32)
    for g in range(groups):
        k = pick(k_scr, g, groups, cuts, tile)
        v = pick(v_scr, g, groups, cuts, tile)
        err = (eta_ref[:, g:g + 1] * v.astype(jnp.float32)).astype(jnp.bfloat16)
        h_one = dot(k, b_ref[g, 0], ((1,), (0,)))
        h_three = dot(k, b_ref[g, 1], ((1,), (0,)))
        back = dot(err, b_ref[g, 2], ((1,), (1,)))
        sig = sigmoid(h_one)
        gate = h_one * sig
        act = (gate * h_three).astype(jnp.bfloat16)
        d_one = (back * h_three * (sig * (1.0 + h_one * (1.0 - sig)))).astype(jnp.bfloat16)
        d_three = (back * gate).astype(jnp.bfloat16)
        acc[g, 0] += dot(k, d_one, ((0,), (0,)))
        acc[g, 1] += dot(k, d_three, ((0,), (0,)))
        acc[g, 2] += dot(act, err, ((0,), (0,)))

    @pl.when(i == pl.num_programs(0) - 1)
    def _():
        out_ref[...] = acc[...].astype(out_ref.dtype)


def local_terms(k_view, v_view, eta_rows, halves):
    groups, kinds, width, feats = halves.shape
    cuts = feats // LANES
    tokens = eta_rows.shape[0]
    tile = min(512, tokens)
    rows = tile * groups * cuts
    whole = pl.BlockSpec(memory_space=pltpu.VMEM)
    return pl.pallas_call(
        functools.partial(terms_kernel, groups, cuts, tile),
        grid=(tokens // tile,),
        out_shape=jax.ShapeDtypeStruct(halves.shape, jnp.bfloat16),
        in_specs=[
            pl.BlockSpec((rows, LANES), lambda i: (i, 0)),
            pl.BlockSpec((rows, LANES), lambda i: (i, 0)),
            pl.BlockSpec((tile, groups), lambda i: (i, 0)),
            whole,
        ],
        out_specs=whole,
        scratch_shapes=[
            pltpu.VMEM((rows, LANES), jnp.float32),
            pltpu.VMEM((rows, LANES), jnp.float32),
            pltpu.VMEM(halves.shape, jnp.float32),
        ],
        compiler_params=pltpu.CompilerParams(vmem_limit_bytes=VMEM_LIMIT),
        name="local_terms",
    )(k_view, v_view, eta_rows, halves)


def apply_kernel(groups, cuts, tile, denom, count_ref, scale_ref, q_ref, c_ref, out_ref, q_scr, o_scr):
    i = pl.program_id(0)
    step = groups * cuts
    position = i * tile + lax.broadcasted_iota(jnp.int32, (tile, 1), 0)
    live = (position < count_ref[0]).astype(jnp.float32)
    q_scr[...] = q_ref[...].astype(jnp.float32)
    pieces = []
    total_sq = jnp.zeros((tile, 1), jnp.float32)
    for g in range(groups):
        q = pick(q_scr, g, groups, cuts, tile)
        q_one = dot(q, c_ref[g, 0], ((1,), (0,)))
        q_three = dot(q, c_ref[g, 1], ((1,), (0,)))
        a_query = (q_one * sigmoid(q_one) * q_three).astype(jnp.bfloat16)
        o = dot(a_query, c_ref[g, 2], ((1,), (0,))).astype(jnp.bfloat16)
        o = o.astype(jnp.float32) * live
        if denom is not None:
            o = o * scale_ref[g]
            total_sq = total_sq + jnp.sum(o * o, axis=-1, keepdims=True)
        pieces.append(o)
    if denom is not None:
        factor = lax.rsqrt(total_sq / denom + EPS)
        pieces = [o * factor for o in pieces]
    for g in range(groups):
        for c in range(cuts):
            o_scr[pl.ds(c * groups + g, tile, stride=step), :] = pieces[g][:, c * LANES:(c + 1) * LANES]
    out_ref[...] = o_scr[...].astype(out_ref.dtype)


def apply_rows(q_view, count, scales, fresh, tokens, denom):
    groups, kinds, width, feats = fresh.shape
    cuts = feats // LANES
    tile = min(512, tokens)
    rows = tile * groups * cuts
    smem = pl.BlockSpec(memory_space=pltpu.SMEM)
    return pl.pallas_call(
        functools.partial(apply_kernel, groups, cuts, tile, denom),
        grid=(tokens // tile,),
        out_shape=jax.ShapeDtypeStruct(q_view.shape, jnp.bfloat16),
        in_specs=[
            smem,
            smem,
            pl.BlockSpec((rows, LANES), lambda i: (i, 0)),
            pl.BlockSpec(memory_space=pltpu.VMEM),
        ],
        out_specs=pl.BlockSpec((rows, LANES), lambda i: (i, 0)),
        scratch_shapes=[
            pltpu.VMEM((rows, LANES), jnp.float32),
            pltpu.VMEM((rows, LANES), jnp.float32),
        ],
        compiler_params=pltpu.CompilerParams(vmem_limit_bytes=VMEM_LIMIT),
        name="apply_rows",
    )(count, scales, q_view, fresh)


def shards(
    queries, key_rows, value_rows, step_rates, live_counts, group_scales, w_first, w_third, w_second
):
    cap_rows, groups, feat_width = queries.shape
    seq_size = lax.axis_size("seq")
    heads = lax.axis_size("heads")
    root_total = jnp.sqrt(jnp.float32(cap_rows * seq_size))
    own_count = lax.dynamic_slice(live_counts, (lax.axis_index("seq"),), (1,))
    live_mask = jnp.arange(cap_rows, dtype=jnp.int32) < own_count[0]
    eta_rows = (
        step_rates.T.astype(jnp.float32) * live_mask.astype(jnp.float32)[:, None] / root_total
    )
    w_own = jnp.stack([w_first, w_third, w_second], axis=1)
    full = (groups, 3, feat_width, feat_width)
    chips = seq_size // 2
    own_rows = w_own.shape[2]
    pieces = w_own.reshape(groups * 3, 1, own_rows, feat_width)
    halves = gather_rows(seq_size, pieces.astype(jnp.bfloat16)).reshape(full)
    part = local_terms(to_view(key_rows), to_view(value_rows), eta_rows, halves)
    part = part.reshape(groups * 3, 1, chips, 2, own_rows, feat_width)
    fresh = reduce_rows(seq_size, part, pieces).reshape(full)
    denom = groups * feat_width * heads
    view = apply_rows(
        to_view(queries), own_count, group_scales, fresh, cap_rows, denom if heads == 1 else None
    )
    fast = from_view(view, queries.shape)
    if heads == 1:
        return fast
    wide = fast.astype(jnp.float32) * group_scales[None, :, None]
    total_sq = lax.psum(jnp.sum(wide * wide, axis=(1, 2)), "heads")
    factor = lax.rsqrt(total_sq / denom + EPS)[:, None, None]
    return (wide * factor).astype(jnp.bfloat16)


def solution(mesh):
    in_specs = (
        P("seq", "heads", None),
        P("seq", "heads", None),
        P("seq", "heads", None),
        P("heads", "seq"),
        P(),
        P("heads"),
        P("heads", "seq", None),
        P("heads", "seq", None),
        P("heads", "seq", None),
    )
    out_specs = P("seq", "heads", None)
    return jax.shard_map(shards, mesh=mesh, in_specs=in_specs, out_specs=out_specs, check_vma=False)
```

```python
import functools

import jax
import jax.numpy as jnp
from jax import lax
from jax.experimental import pallas as pl
from jax.experimental.pallas import tpu as pltpu
from jax.sharding import PartitionSpec as P

EPS = 1e-06
MESH = pl.DeviceIdType.MESH
LANES = 128
VMEM_LIMIT = 60 * 1024 * 1024


class Grid:
    def __init__(self, n):
        me = lax.axis_index("seq")
        self.depth = n // 8
        self.core = me % 2
        self.x = (me // 2) % 2
        self.y = (me // 4) % 2
        self.z = me // 8
        self.partner = self.index(self.z, self.y, self.x, 1 - self.core)

    def index(self, z, y, x, core):
        return z * 8 + y * 4 + x * 2 + core

    def place(self, half, near, far):
        flip_y, flip_x = (far, near) if half == 0 else (near, far)
        return (1 - self.y if flip_y else self.y), (1 - self.x if flip_x else self.x)

    def peer(self, half, near, far):
        y, x = self.place(half, near, far)
        return self.index(self.z, y, x, self.core)

    def column(self, step):
        return (self.z + step + self.depth) % self.depth

    def z_peer(self, step):
        return self.index(self.column(step), self.y, self.x, self.core)

    def barrier(self):
        sem = pltpu.get_barrier_semaphore()
        peers = [self.z_peer(k) for k in range(1, self.depth)]
        peers += [self.peer(0, 1, 0), self.peer(0, 0, 1), self.partner]
        for peer in peers:
            pl.semaphore_signal(sem, inc=1, device_id={"seq": peer}, device_id_type=MESH)
        pl.semaphore_wait(sem, len(peers))


def remote(src, dst, send_sem, recv_sem, peer):
    return pltpu.make_async_remote_copy(
        src_ref=src, dst_ref=dst, send_sem=send_sem, recv_sem=recv_sem,
        device_id={"seq": peer}, device_id_type=MESH,
    )


def gather_blocks(grid, own, out, sems):
    zs, zr, ns, nr, fs, fr, ps, pr = sems
    depth = grid.depth
    started = []
    partners = []

    def slot(half, k, near, far):
        y, x = grid.place(half, near, far)
        return out.at[half, :, grid.column(-k), y, x, grid.core]

    def source(half, k, near, far):
        return own.at[half] if (k, near, far) == (0, 0, 0) else slot(half, k, near, far)

    def send(copy):
        copy.start()
        started.append(copy)
        return copy

    def to_near(half, k):
        return remote(source(half, k, 0, 0), slot(half, k, 0, 0),
                      ns.at[half, k], nr.at[half, k], grid.peer(half, 1, 0))

    def to_far(half, k, near):
        return remote(source(half, k, near, 0), slot(half, k, near, 0),
                      fs.at[half, near, k], fr.at[half, near, k], grid.peer(half, 0, 1))

    def to_partner(half, k, near, far):
        copy = remote(source(half, k, near, far), slot(half, k, near, far),
                      ps.at[half, near, far, k], pr.at[half, near, far, k], grid.partner)
        partners.append(send(copy))

    columns = {}
    for k in range(1, depth):
        for half in range(2):
            columns[half, k] = send(remote(own.at[half], slot(half, 0, 0, 0), zs.at[half, k - 1],
                                           zr.at[half, k - 1], grid.z_peer(k)))
    for half in range(2):
        out[half, :, grid.z, grid.y, grid.x, grid.core] = own[half]
    nears, fars = {}, {}
    order = [0] + [k for d in range(1, depth) for k in (d, depth - d) if d <= depth - d]
    order = list(dict.fromkeys(order))
    for i in range(depth + 1):
        for half in range(2):
            if i < depth:
                k = order[i]
                if k > 0:
                    columns[half, k].wait_recv()
                nears[half, k] = send(to_near(half, k))
                fars[half, 0, k] = send(to_far(half, k, 0))
                to_partner(half, k, 0, 0)
            if i > 0:
                k = order[i - 1]
                nears[half, k].wait_recv()
                fars[half, 1, k] = send(to_far(half, k, 1))
                to_partner(half, k, 1, 0)
    for k in order:
        for half in range(2):
            for near in range(2):
                fars[half, near, k].wait_recv()
                to_partner(half, k, near, 1)
    for copy in partners:
        copy.wait_recv()
    for copy in started:
        copy.wait_send()


def gather_sems(n):
    depth = n // 8
    dma = pltpu.SemaphoreType.DMA
    sems = []
    for shape in ((2, max(depth - 1, 1)), (2, depth), (2, 2, depth), (2, 2, 2, depth)):
        sems += [dma(shape), dma(shape)]
    return sems


def gather_kernel(n, own_ref, out_ref, *sems):
    grid = Grid(n)
    grid.barrier()
    gather_blocks(grid, own_ref, out_ref, sems)


def gather_rows(n, own):
    halves, kinds, rows, feats = own.shape
    return pl.pallas_call(
        functools.partial(gather_kernel, n),
        out_shape=jax.ShapeDtypeStruct((halves, kinds, n // 8, 2, 2, 2, rows, feats), own.dtype),
        in_specs=[pl.BlockSpec(memory_space=pltpu.VMEM)],
        out_specs=pl.BlockSpec(memory_space=pltpu.VMEM),
        scratch_shapes=gather_sems(n),
        compiler_params=pltpu.CompilerParams(
            collective_id=0, has_side_effects=True, vmem_limit_bytes=VMEM_LIMIT
        ),
        name="gather_start",
    )(own)


def reduce_kernel(n, part_ref, w_ref, out_ref, pair_in, far_out, far_in, near_out, near_in,
                  z_out, z_in, fresh, xs, xr, fs, fr, ns, nr, zs, zr, *gsems):
    grid = Grid(n)
    depth = grid.depth
    f32 = jnp.float32
    grid.barrier()
    order = list(range(1, depth)) + [0]
    started = []

    def send(copy):
        copy.start()
        started.append(copy)
        return copy

    exchange, fars, nears, columns = {}, {}, {}, {}
    for k in order:
        for half in range(2):
            col = grid.column(k)
            exchange[half, k] = send(remote(
                part_ref.at[half, :, col, :, :, 1 - grid.core], pair_in.at[half, :, k],
                xs.at[half, k], xr.at[half, k], grid.partner))

    def both(half, k, near, far):
        y, x = grid.place(half, near, far)
        return (part_ref[half, :, grid.column(k), y, x, grid.core].astype(f32)
                + pair_in[half, :, k, y, x].astype(f32))

    for k in order:
        for half in range(2):
            exchange[half, k].wait_recv()
            for near in range(2):
                far_out[half, k, near] = both(half, k, near, 1).astype(far_out.dtype)
            fars[half, k] = send(remote(far_out.at[half, k], far_in.at[half, k],
                                        fs.at[half, k], fr.at[half, k], grid.peer(half, 0, 1)))
    for k in order:
        for half in range(2):
            fars[half, k].wait_recv()
            near_out[half, k] = (both(half, k, 1, 0) + far_in[half, k, 1].astype(f32)
                                 ).astype(near_out.dtype)
            nears[half, k] = send(remote(near_out.at[half, k], near_in.at[half, k],
                                         ns.at[half, k], nr.at[half, k], grid.peer(half, 1, 0)))
    totals = [None, None]
    for k in order:
        for half in range(2):
            nears[half, k].wait_recv()
            value = (both(half, k, 0, 0) + far_in[half, k, 0].astype(f32)
                     + near_in[half, k].astype(f32))
            if k == 0:
                totals[half] = value
            else:
                z_out[half, k - 1] = value.astype(z_out.dtype)
                columns[half, k] = send(remote(z_out.at[half, k - 1], z_in.at[half, k - 1],
                                               zs.at[half, k - 1], zr.at[half, k - 1],
                                               grid.z_peer(k)))
    for half in range(2):
        term = totals[half]
        for k in range(1, depth):
            columns[half, k].wait_recv()
            term = term + z_in[half, k - 1].astype(f32)
        start_w = w_ref[half]
        update = start_w + term
        norm_old = jnp.sqrt(jnp.mean(start_w * start_w, axis=-1, keepdims=True) + EPS)
        norm_new = jnp.sqrt(jnp.mean(update * update, axis=-1, keepdims=True) + EPS)
        fresh[half] = (update * (norm_old / norm_new)).astype(fresh.dtype)

    gather_blocks(grid, fresh, out_ref, gsems)
    for copy in started:
        copy.wait_send()


def reduce_rows(n, part, w_own):
    halves, kinds, rows, feats = w_own.shape
    depth = n // 8
    hops = max(depth - 1, 1)
    dma = pltpu.SemaphoreType.DMA
    bf = jnp.bfloat16
    block = (kinds, rows, feats)
    return pl.pallas_call(
        functools.partial(reduce_kernel, n),
        out_shape=jax.ShapeDtypeStruct((halves, kinds, depth, 2, 2, 2, rows, feats), bf),
        in_specs=[pl.BlockSpec(memory_space=pltpu.VMEM)] * 2,
        out_specs=pl.BlockSpec(memory_space=pltpu.VMEM),
        scratch_shapes=[
            pltpu.VMEM((halves, kinds, depth, 2, 2, rows, feats), bf),
            pltpu.VMEM((halves, depth, 2) + block, bf),
            pltpu.VMEM((halves, depth, 2) + block, bf),
            pltpu.VMEM((halves, depth) + block, bf),
            pltpu.VMEM((halves, depth) + block, bf),
            pltpu.VMEM((halves, hops) + block, bf),
            pltpu.VMEM((halves, hops) + block, bf),
            pltpu.VMEM((halves,) + block, bf),
            dma((2, depth)), dma((2, depth)), dma((2, depth)), dma((2, depth)),
            dma((2, depth)), dma((2, depth)), dma((2, hops)), dma((2, hops)),
        ] + gather_sems(n),
        compiler_params=pltpu.CompilerParams(
            collective_id=1, has_side_effects=True, vmem_limit_bytes=VMEM_LIMIT
        ),
        name="reduce_gather",
    )(part, w_own)


def to_view(rows):
    tokens, groups, feats = rows.shape
    cuts = feats // LANES
    return rows.reshape(tokens, groups, cuts, LANES).transpose(0, 2, 1, 3).reshape(-1, LANES)


def from_view(view, shape):
    tokens, groups, feats = shape
    cuts = feats // LANES
    return view.reshape(tokens, cuts, groups, LANES).transpose(0, 2, 1, 3).reshape(shape)


def pick(scr, g, groups, cuts, tile):
    step = groups * cuts
    cols = [scr[pl.ds(c * groups + g, tile, stride=step), :] for c in range(cuts)]
    return jnp.concatenate(cols, axis=-1).astype(jnp.bfloat16)


def dot(a, b, dims):
    return lax.dot_general(a, b, (dims, ((), ())), preferred_element_type=jnp.float32)


def sigmoid(x):
    return 0.5 * jnp.tanh(0.5 * x) + 0.5


def terms_kernel(groups, cuts, tile, k_ref, v_ref, eta_ref, b_ref, out_ref, k_scr, v_scr, acc):
    i = pl.program_id(0)

    @pl.when(i == 0)
    def _():
        acc[...] = jnp.zeros_like(acc)

    k_scr[...] = k_ref[...].astype(jnp.float32)
    v_scr[...] = v_ref[...].astype(jnp.float32)
    for g in range(groups):
        k = pick(k_scr, g, groups, cuts, tile)
        v = pick(v_scr, g, groups, cuts, tile)
        err = (eta_ref[:, g:g + 1] * v.astype(jnp.float32)).astype(jnp.bfloat16)
        h_one = dot(k, b_ref[g, 0], ((1,), (0,)))
        h_three = dot(k, b_ref[g, 1], ((1,), (0,)))
        back = dot(err, b_ref[g, 2], ((1,), (1,)))
        sig = sigmoid(h_one)
        gate = h_one * sig
        act = (gate * h_three).astype(jnp.bfloat16)
        d_one = (back * h_three * (sig * (1.0 + h_one * (1.0 - sig)))).astype(jnp.bfloat16)
        d_three = (back * gate).astype(jnp.bfloat16)
        acc[g, 0] += dot(k, d_one, ((0,), (0,)))
        acc[g, 1] += dot(k, d_three, ((0,), (0,)))
        acc[g, 2] += dot(act, err, ((0,), (0,)))

    @pl.when(i == pl.num_programs(0) - 1)
    def _():
        out_ref[...] = acc[...].astype(out_ref.dtype)


def local_terms(k_view, v_view, eta_rows, halves):
    groups, kinds, width, feats = halves.shape
    cuts = feats // LANES
    tokens = eta_rows.shape[0]
    tile = min(512, tokens)
    rows = tile * groups * cuts
    whole = pl.BlockSpec(memory_space=pltpu.VMEM)
    return pl.pallas_call(
        functools.partial(terms_kernel, groups, cuts, tile),
        grid=(tokens // tile,),
        out_shape=jax.ShapeDtypeStruct(halves.shape, jnp.bfloat16),
        in_specs=[
            pl.BlockSpec((rows, LANES), lambda i: (i, 0)),
            pl.BlockSpec((rows, LANES), lambda i: (i, 0)),
            pl.BlockSpec((tile, groups), lambda i: (i, 0)),
            whole,
        ],
        out_specs=whole,
        scratch_shapes=[
            pltpu.VMEM((rows, LANES), jnp.float32),
            pltpu.VMEM((rows, LANES), jnp.float32),
            pltpu.VMEM(halves.shape, jnp.float32),
        ],
        compiler_params=pltpu.CompilerParams(vmem_limit_bytes=VMEM_LIMIT),
        name="local_terms",
    )(k_view, v_view, eta_rows, halves)


def apply_kernel(groups, cuts, tile, denom, count_ref, scale_ref, q_ref, c_ref, out_ref, q_scr, o_scr):
    i = pl.program_id(0)
    step = groups * cuts
    position = i * tile + lax.broadcasted_iota(jnp.int32, (tile, 1), 0)
    live = (position < count_ref[0]).astype(jnp.float32)
    q_scr[...] = q_ref[...].astype(jnp.float32)
    pieces = []
    total_sq = jnp.zeros((tile, 1), jnp.float32)
    for g in range(groups):
        q = pick(q_scr, g, groups, cuts, tile)
        q_one = dot(q, c_ref[g, 0], ((1,), (0,)))
        q_three = dot(q, c_ref[g, 1], ((1,), (0,)))
        a_query = (q_one * sigmoid(q_one) * q_three).astype(jnp.bfloat16)
        o = dot(a_query, c_ref[g, 2], ((1,), (0,))).astype(jnp.bfloat16)
        o = o.astype(jnp.float32) * live
        if denom is not None:
            o = o * scale_ref[g]
            total_sq = total_sq + jnp.sum(o * o, axis=-1, keepdims=True)
        pieces.append(o)
    if denom is not None:
        factor = lax.rsqrt(total_sq / denom + EPS)
        pieces = [o * factor for o in pieces]
    for g in range(groups):
        for c in range(cuts):
            o_scr[pl.ds(c * groups + g, tile, stride=step), :] = pieces[g][:, c * LANES:(c + 1) * LANES]
    out_ref[...] = o_scr[...].astype(out_ref.dtype)


def apply_rows(q_view, count, scales, fresh, tokens, denom):
    groups, kinds, width, feats = fresh.shape
    cuts = feats // LANES
    tile = min(512, tokens)
    rows = tile * groups * cuts
    smem = pl.BlockSpec(memory_space=pltpu.SMEM)
    return pl.pallas_call(
        functools.partial(apply_kernel, groups, cuts, tile, denom),
        grid=(tokens // tile,),
        out_shape=jax.ShapeDtypeStruct(q_view.shape, jnp.bfloat16),
        in_specs=[
            smem,
            smem,
            pl.BlockSpec((rows, LANES), lambda i: (i, 0)),
            pl.BlockSpec(memory_space=pltpu.VMEM),
        ],
        out_specs=pl.BlockSpec((rows, LANES), lambda i: (i, 0)),
        scratch_shapes=[
            pltpu.VMEM((rows, LANES), jnp.float32),
            pltpu.VMEM((rows, LANES), jnp.float32),
        ],
        compiler_params=pltpu.CompilerParams(vmem_limit_bytes=VMEM_LIMIT),
        name="apply_rows",
    )(count, scales, q_view, fresh)


def shards(
    queries, key_rows, value_rows, step_rates, live_counts, group_scales, w_first, w_third, w_second
):
    cap_rows, groups, feat_width = queries.shape
    seq_size = lax.axis_size("seq")
    heads = lax.axis_size("heads")
    root_total = jnp.sqrt(jnp.float32(cap_rows * seq_size))
    own_count = lax.dynamic_slice(live_counts, (lax.axis_index("seq"),), (1,))
    live_mask = jnp.arange(cap_rows, dtype=jnp.int32) < own_count[0]
    eta_rows = (
        step_rates.T.astype(jnp.float32) * live_mask.astype(jnp.float32)[:, None] / root_total
    )
    w_own = jnp.stack([w_first, w_third, w_second], axis=1)
    full = (groups, 3, feat_width, feat_width)
    own_rows = w_own.shape[2]
    pieces = w_own.reshape(2, groups * 3 // 2, own_rows, feat_width)
    halves = gather_rows(seq_size, pieces.astype(jnp.bfloat16)).reshape(full)
    part = local_terms(to_view(key_rows), to_view(value_rows), eta_rows, halves)
    part = part.reshape(2, groups * 3 // 2, seq_size // 8, 2, 2, 2, own_rows, feat_width)
    fresh = reduce_rows(seq_size, part, pieces).reshape(full)
    denom = groups * feat_width * heads
    view = apply_rows(
        to_view(queries), own_count, group_scales, fresh, cap_rows, denom if heads == 1 else None
    )
    fast = from_view(view, queries.shape)
    if heads == 1:
        return fast
    wide = fast.astype(jnp.float32) * group_scales[None, :, None]
    total_sq = lax.psum(jnp.sum(wide * wide, axis=(1, 2)), "heads")
    factor = lax.rsqrt(total_sq / denom + EPS)[:, None, None]
    return (wide * factor).astype(jnp.bfloat16)


def solution(mesh):
    in_specs = (
        P("seq", "heads", None),
        P("seq", "heads", None),
        P("seq", "heads", None),
        P("heads", "seq"),
        P(),
        P("heads"),
        P("heads", "seq", None),
        P("heads", "seq", None),
        P("heads", "seq", None),
    )
    out_specs = P("seq", "heads", None)
    return jax.shard_map(shards, mesh=mesh, in_specs=in_specs, out_specs=out_specs, check_vma=False)
```

```python
import functools
import math

import jax
import jax.numpy as jnp
from jax import lax
from jax.experimental import pallas as pl
from jax.experimental.pallas import tpu as pltpu
from jax.sharding import PartitionSpec as P

EPS = 1e-06
MESH = pl.DeviceIdType.MESH
LANES = 128
VMEM_LIMIT = 60 * 1024 * 1024


class Grid:
    def __init__(self, n):
        me = lax.axis_index("seq")
        self.depth = n // 8
        self.core = me % 2
        self.x = (me // 2) % 2
        self.y = (me // 4) % 2
        self.z = me // 8
        self.partner = self.index(self.z, self.y, self.x, 1 - self.core)

    def index(self, z, y, x, core):
        return z * 8 + y * 4 + x * 2 + core

    def place(self, half, near, far):
        flip_y, flip_x = (far, near) if half == 0 else (near, far)
        return (1 - self.y if flip_y else self.y), (1 - self.x if flip_x else self.x)

    def peer(self, half, near, far):
        y, x = self.place(half, near, far)
        return self.index(self.z, y, x, self.core)

    def column(self, step):
        return (self.z + step + self.depth) % self.depth

    def z_peer(self, step):
        return self.index(self.column(step), self.y, self.x, self.core)

    def barrier(self):
        sem = pltpu.get_barrier_semaphore()
        peers = [self.z_peer(k) for k in range(1, self.depth)]
        peers += [self.peer(0, 1, 0), self.peer(0, 0, 1), self.partner]
        for peer in peers:
            pl.semaphore_signal(sem, inc=1, device_id={"seq": peer}, device_id_type=MESH)
        pl.semaphore_wait(sem, len(peers))


def remote(src, dst, send_sem, recv_sem, peer):
    return pltpu.make_async_remote_copy(
        src_ref=src, dst_ref=dst, send_sem=send_sem, recv_sem=recv_sem,
        device_id={"seq": peer}, device_id_type=MESH,
    )


def gather_blocks(grid, own, out, sems):
    zs, zr, ns, nr, fs, fr, ps, pr = sems
    depth = grid.depth
    started = []
    partners = []

    def slot(half, k, near, far):
        y, x = grid.place(half, near, far)
        return out.at[half, :, grid.column(-k), y, x, grid.core]

    def source(half, k, near, far):
        return own.at[half] if (k, near, far) == (0, 0, 0) else slot(half, k, near, far)

    def send(copy):
        copy.start()
        started.append(copy)
        return copy

    def to_near(half, k):
        return remote(source(half, k, 0, 0), slot(half, k, 0, 0),
                      ns.at[half, k], nr.at[half, k], grid.peer(half, 1, 0))

    def to_far(half, k, near):
        return remote(source(half, k, near, 0), slot(half, k, near, 0),
                      fs.at[half, near, k], fr.at[half, near, k], grid.peer(half, 0, 1))

    def to_partner(half, k, near, far):
        copy = remote(source(half, k, near, far), slot(half, k, near, far),
                      ps.at[half, near, far, k], pr.at[half, near, far, k], grid.partner)
        partners.append(send(copy))

    columns = {}
    for k in range(1, depth):
        for half in range(2):
            columns[half, k] = send(remote(own.at[half], slot(half, 0, 0, 0), zs.at[half, k - 1],
                                           zr.at[half, k - 1], grid.z_peer(k)))
    for half in range(2):
        out[half, :, grid.z, grid.y, grid.x, grid.core] = own[half]
    nears, fars = {}, {}
    order = [0] + [k for d in range(1, depth) for k in (d, depth - d) if d <= depth - d]
    order = list(dict.fromkeys(order))
    for i in range(depth + 1):
        for half in range(2):
            if i < depth:
                k = order[i]
                if k > 0:
                    columns[half, k].wait_recv()
                nears[half, k] = send(to_near(half, k))
                fars[half, 0, k] = send(to_far(half, k, 0))
                to_partner(half, k, 0, 0)
            if i > 0:
                k = order[i - 1]
                nears[half, k].wait_recv()
                fars[half, 1, k] = send(to_far(half, k, 1))
                to_partner(half, k, 1, 0)
    for k in order:
        for half in range(2):
            for near in range(2):
                fars[half, near, k].wait_recv()
                to_partner(half, k, near, 1)
    for copy in partners:
        copy.wait_recv()
    for copy in started:
        copy.wait_send()


def gather_sems(n):
    depth = n // 8
    dma = pltpu.SemaphoreType.DMA
    sems = []
    for shape in ((2, max(depth - 1, 1)), (2, depth), (2, 2, depth), (2, 2, 2, depth)):
        sems += [dma(shape), dma(shape)]
    return sems


def gather_kernel(n, own_ref, out_ref, *sems):
    grid = Grid(n)
    grid.barrier()
    gather_blocks(grid, own_ref, out_ref, sems)


def gather_rows(n, own):
    halves, kinds, rows, feats = own.shape
    return pl.pallas_call(
        functools.partial(gather_kernel, n),
        out_shape=jax.ShapeDtypeStruct((halves, kinds, n // 8, 2, 2, 2, rows, feats), own.dtype),
        in_specs=[pl.BlockSpec(memory_space=pltpu.VMEM)],
        out_specs=pl.BlockSpec(memory_space=pltpu.VMEM),
        scratch_shapes=gather_sems(n),
        compiler_params=pltpu.CompilerParams(
            collective_id=0, has_side_effects=True, vmem_limit_bytes=VMEM_LIMIT
        ),
        name="gather_start",
    )(own)


def reduce_kernel(n, part_ref, w_ref, out_ref, pair_in, far_out, far_in, near_out, near_in,
                  z_out, z_in, fresh, xs, xr, fs, fr, ns, nr, zs, zr, *gsems):
    grid = Grid(n)
    depth = grid.depth
    f32 = jnp.float32
    grid.barrier()
    order = list(range(1, depth)) + [0]
    started = []

    def send(copy):
        copy.start()
        started.append(copy)
        return copy

    exchange, fars, nears, columns = {}, {}, {}, {}
    for k in order:
        for half in range(2):
            col = grid.column(k)
            exchange[half, k] = send(remote(
                part_ref.at[half, :, col, :, :, 1 - grid.core], pair_in.at[half, :, k],
                xs.at[half, k], xr.at[half, k], grid.partner))

    def both(half, k, near, far):
        y, x = grid.place(half, near, far)
        return (part_ref[half, :, grid.column(k), y, x, grid.core].astype(f32)
                + pair_in[half, :, k, y, x].astype(f32))

    for k in order:
        for half in range(2):
            exchange[half, k].wait_recv()
            for near in range(2):
                far_out[half, k, near] = both(half, k, near, 1).astype(far_out.dtype)
            fars[half, k] = send(remote(far_out.at[half, k], far_in.at[half, k],
                                        fs.at[half, k], fr.at[half, k], grid.peer(half, 0, 1)))
    for k in order:
        for half in range(2):
            fars[half, k].wait_recv()
            near_out[half, k] = (both(half, k, 1, 0) + far_in[half, k, 1].astype(f32)
                                 ).astype(near_out.dtype)
            nears[half, k] = send(remote(near_out.at[half, k], near_in.at[half, k],
                                         ns.at[half, k], nr.at[half, k], grid.peer(half, 1, 0)))
    totals = [None, None]
    for k in order:
        for half in range(2):
            nears[half, k].wait_recv()
            value = (both(half, k, 0, 0) + far_in[half, k, 0].astype(f32)
                     + near_in[half, k].astype(f32))
            if k == 0:
                totals[half] = value
            else:
                z_out[half, k - 1] = value.astype(z_out.dtype)
                columns[half, k] = send(remote(z_out.at[half, k - 1], z_in.at[half, k - 1],
                                               zs.at[half, k - 1], zr.at[half, k - 1],
                                               grid.z_peer(k)))
    for half in range(2):
        term = totals[half]
        for k in range(1, depth):
            columns[half, k].wait_recv()
            term = term + z_in[half, k - 1].astype(f32)
        start_w = w_ref[half]
        update = start_w + term
        norm_old = jnp.sqrt(jnp.mean(start_w * start_w, axis=-1, keepdims=True) + EPS)
        norm_new = jnp.sqrt(jnp.mean(update * update, axis=-1, keepdims=True) + EPS)
        fresh[half] = (update * (norm_old / norm_new)).astype(fresh.dtype)

    gather_blocks(grid, fresh, out_ref, gsems)
    for copy in started:
        copy.wait_send()


def reduce_rows(n, part, w_own):
    halves, kinds, rows, feats = w_own.shape
    depth = n // 8
    hops = max(depth - 1, 1)
    dma = pltpu.SemaphoreType.DMA
    bf = jnp.bfloat16
    block = (kinds, rows, feats)
    return pl.pallas_call(
        functools.partial(reduce_kernel, n),
        out_shape=jax.ShapeDtypeStruct((halves, kinds, depth, 2, 2, 2, rows, feats), bf),
        in_specs=[pl.BlockSpec(memory_space=pltpu.VMEM)] * 2,
        out_specs=pl.BlockSpec(memory_space=pltpu.VMEM),
        scratch_shapes=[
            pltpu.VMEM((halves, kinds, depth, 2, 2, rows, feats), bf),
            pltpu.VMEM((halves, depth, 2) + block, bf),
            pltpu.VMEM((halves, depth, 2) + block, bf),
            pltpu.VMEM((halves, depth) + block, bf),
            pltpu.VMEM((halves, depth) + block, bf),
            pltpu.VMEM((halves, hops) + block, bf),
            pltpu.VMEM((halves, hops) + block, bf),
            pltpu.VMEM((halves,) + block, bf),
            dma((2, depth)), dma((2, depth)), dma((2, depth)), dma((2, depth)),
            dma((2, depth)), dma((2, depth)), dma((2, hops)), dma((2, hops)),
        ] + gather_sems(n),
        compiler_params=pltpu.CompilerParams(
            collective_id=1, has_side_effects=True, vmem_limit_bytes=VMEM_LIMIT
        ),
        name="reduce_gather",
    )(part, w_own)


def to_view(rows):
    tokens, groups, feats = rows.shape
    cuts = feats // LANES
    return rows.reshape(tokens, groups, cuts, LANES).transpose(0, 2, 1, 3).reshape(-1, LANES)


def from_view(view, shape):
    tokens, groups, feats = shape
    cuts = feats // LANES
    return view.reshape(tokens, cuts, groups, LANES).transpose(0, 2, 1, 3).reshape(shape)


def pick(scr, g, groups, cuts, tile):
    step = groups * cuts
    cols = [scr[pl.ds(c * groups + g, tile, stride=step), :] for c in range(cuts)]
    return jnp.concatenate(cols, axis=-1).astype(jnp.bfloat16)


def dot(a, b, dims):
    return lax.dot_general(a, b, (dims, ((), ())), preferred_element_type=jnp.float32)


def sigmoid(x):
    return 0.5 * jnp.tanh(0.5 * x) + 0.5


def terms_kernel(groups, cuts, tile, root, count_ref, k_ref, v_ref, rate_ref, b_ref, out_ref, k_scr, v_scr, acc):
    i = pl.program_id(0)

    @pl.when(i == 0)
    def _():
        acc[...] = jnp.zeros_like(acc)

    position = i * tile + lax.broadcasted_iota(jnp.int32, (tile, 1), 0)
    live = (position < count_ref[lax.axis_index("seq")]).astype(jnp.float32)
    rates = rate_ref[...].astype(jnp.float32)
    k_scr[...] = k_ref[...].astype(jnp.float32)
    v_scr[...] = v_ref[...].astype(jnp.float32)
    for g in range(groups):
        k = pick(k_scr, g, groups, cuts, tile)
        v = pick(v_scr, g, groups, cuts, tile)
        column = jnp.broadcast_to(rates[g:g + 1], (8, tile)).T[:, 0:1]
        eta = column * live / root
        err = (eta * v.astype(jnp.float32)).astype(jnp.bfloat16)
        h_one = dot(k, b_ref[g, 0], ((1,), (0,)))
        h_three = dot(k, b_ref[g, 1], ((1,), (0,)))
        back = dot(err, b_ref[g, 2], ((1,), (1,)))
        sig = sigmoid(h_one)
        gate = h_one * sig
        act = (gate * h_three).astype(jnp.bfloat16)
        d_one = (back * h_three * (sig * (1.0 + h_one * (1.0 - sig)))).astype(jnp.bfloat16)
        d_three = (back * gate).astype(jnp.bfloat16)
        acc[g, 0] += dot(k, d_one, ((0,), (0,)))
        acc[g, 1] += dot(k, d_three, ((0,), (0,)))
        acc[g, 2] += dot(act, err, ((0,), (0,)))

    @pl.when(i == pl.num_programs(0) - 1)
    def _():
        out_ref[...] = acc[...].astype(out_ref.dtype)


def local_terms(k_view, v_view, rates, counts, halves, root):
    groups, kinds, width, feats = halves.shape
    cuts = feats // LANES
    tokens = rates.shape[1]
    tile = min(512, tokens)
    rows = tile * groups * cuts
    whole = pl.BlockSpec(memory_space=pltpu.VMEM)
    return pl.pallas_call(
        functools.partial(terms_kernel, groups, cuts, tile, root),
        grid=(tokens // tile,),
        out_shape=jax.ShapeDtypeStruct(halves.shape, jnp.bfloat16),
        in_specs=[
            pl.BlockSpec(memory_space=pltpu.SMEM),
            pl.BlockSpec((rows, LANES), lambda i: (i, 0)),
            pl.BlockSpec((rows, LANES), lambda i: (i, 0)),
            pl.BlockSpec((groups, tile), lambda i: (0, i)),
            whole,
        ],
        out_specs=whole,
        scratch_shapes=[
            pltpu.VMEM((rows, LANES), jnp.float32),
            pltpu.VMEM((rows, LANES), jnp.float32),
            pltpu.VMEM(halves.shape, jnp.float32),
        ],
        compiler_params=pltpu.CompilerParams(vmem_limit_bytes=VMEM_LIMIT),
        name="local_terms",
    )(counts, k_view, v_view, rates, halves)


def apply_kernel(groups, cuts, tile, denom, count_ref, scale_ref, q_ref, c_ref, out_ref, q_scr, o_scr):
    i = pl.program_id(0)
    step = groups * cuts
    position = i * tile + lax.broadcasted_iota(jnp.int32, (tile, 1), 0)
    live = (position < count_ref[lax.axis_index("seq")]).astype(jnp.float32)
    q_scr[...] = q_ref[...].astype(jnp.float32)
    pieces = []
    total_sq = jnp.zeros((tile, 1), jnp.float32)
    for g in range(groups):
        q = pick(q_scr, g, groups, cuts, tile)
        q_one = dot(q, c_ref[g, 0], ((1,), (0,)))
        q_three = dot(q, c_ref[g, 1], ((1,), (0,)))
        a_query = (q_one * sigmoid(q_one) * q_three).astype(jnp.bfloat16)
        o = dot(a_query, c_ref[g, 2], ((1,), (0,))).astype(jnp.bfloat16)
        o = o.astype(jnp.float32) * live
        if denom is not None:
            o = o * scale_ref[g]
            total_sq = total_sq + jnp.sum(o * o, axis=-1, keepdims=True)
        pieces.append(o)
    if denom is not None:
        factor = lax.rsqrt(total_sq / denom + EPS)
        pieces = [o * factor for o in pieces]
    for g in range(groups):
        for c in range(cuts):
            o_scr[pl.ds(c * groups + g, tile, stride=step), :] = pieces[g][:, c * LANES:(c + 1) * LANES]
    out_ref[...] = o_scr[...].astype(out_ref.dtype)


def apply_rows(q_view, count, scales, fresh, tokens, denom):
    groups, kinds, width, feats = fresh.shape
    cuts = feats // LANES
    tile = min(512, tokens)
    rows = tile * groups * cuts
    smem = pl.BlockSpec(memory_space=pltpu.SMEM)
    return pl.pallas_call(
        functools.partial(apply_kernel, groups, cuts, tile, denom),
        grid=(tokens // tile,),
        out_shape=jax.ShapeDtypeStruct(q_view.shape, jnp.bfloat16),
        in_specs=[
            smem,
            smem,
            pl.BlockSpec((rows, LANES), lambda i: (i, 0)),
            pl.BlockSpec(memory_space=pltpu.VMEM),
        ],
        out_specs=pl.BlockSpec((rows, LANES), lambda i: (i, 0)),
        scratch_shapes=[
            pltpu.VMEM((rows, LANES), jnp.float32),
            pltpu.VMEM((rows, LANES), jnp.float32),
        ],
        compiler_params=pltpu.CompilerParams(vmem_limit_bytes=VMEM_LIMIT),
        name="apply_rows",
    )(count, scales, q_view, fresh)


def shards(
    queries, key_rows, value_rows, step_rates, live_counts, group_scales, w_first, w_third, w_second
):
    cap_rows, groups, feat_width = queries.shape
    seq_size = lax.axis_size("seq")
    heads = lax.axis_size("heads")
    root_total = math.sqrt(cap_rows * seq_size)
    w_own = jnp.stack([w_first, w_third, w_second], axis=1)
    full = (groups, 3, feat_width, feat_width)
    own_rows = w_own.shape[2]
    pieces = w_own.reshape(2, groups * 3 // 2, own_rows, feat_width)
    halves = gather_rows(seq_size, pieces.astype(jnp.bfloat16)).reshape(full)
    part = local_terms(
        to_view(key_rows), to_view(value_rows), step_rates, live_counts, halves, root_total
    )
    part = part.reshape(2, groups * 3 // 2, seq_size // 8, 2, 2, 2, own_rows, feat_width)
    fresh = reduce_rows(seq_size, part, pieces).reshape(full)
    denom = groups * feat_width * heads
    view = apply_rows(
        to_view(queries), live_counts, group_scales, fresh, cap_rows, denom if heads == 1 else None
    )
    fast = from_view(view, queries.shape)
    if heads == 1:
        return fast
    wide = fast.astype(jnp.float32) * group_scales[None, :, None]
    total_sq = lax.psum(jnp.sum(wide * wide, axis=(1, 2)), "heads")
    factor = lax.rsqrt(total_sq / denom + EPS)[:, None, None]
    return (wide * factor).astype(jnp.bfloat16)


def solution(mesh):
    in_specs = (
        P("seq", "heads", None),
        P("seq", "heads", None),
        P("seq", "heads", None),
        P("heads", "seq"),
        P(),
        P("heads"),
        P("heads", "seq", None),
        P("heads", "seq", None),
        P("heads", "seq", None),
    )
    out_specs = P("seq", "heads", None)
    return jax.shard_map(shards, mesh=mesh, in_specs=in_specs, out_specs=out_specs, check_vma=False)
```

```python
import functools
import math

import jax
import jax.numpy as jnp
from jax import lax
from jax.experimental import pallas as pl
from jax.experimental.pallas import tpu as pltpu
from jax.sharding import PartitionSpec as P

EPS = 1e-06
MESH = pl.DeviceIdType.MESH
LANES = 128
VMEM_LIMIT = 60 * 1024 * 1024


class Grid:
    def __init__(self, n):
        me = lax.axis_index("seq")
        self.depth = n // 8
        self.core = me % 2
        self.x = (me // 2) % 2
        self.y = (me // 4) % 2
        self.z = me // 8
        self.partner = self.index(self.z, self.y, self.x, 1 - self.core)

    def index(self, z, y, x, core):
        return z * 8 + y * 4 + x * 2 + core

    def place(self, half, near, far):
        flip_y, flip_x = (far, near) if half == 0 else (near, far)
        return (1 - self.y if flip_y else self.y), (1 - self.x if flip_x else self.x)

    def peer(self, half, near, far):
        y, x = self.place(half, near, far)
        return self.index(self.z, y, x, self.core)

    def column(self, step):
        return (self.z + step + self.depth) % self.depth

    def z_peer(self, step):
        return self.index(self.column(step), self.y, self.x, self.core)

    def barrier(self):
        sem = pltpu.get_barrier_semaphore()
        peers = [self.z_peer(k) for k in range(1, self.depth)]
        peers += [self.peer(0, 1, 0), self.peer(0, 0, 1), self.partner]
        for peer in peers:
            pl.semaphore_signal(sem, inc=1, device_id={"seq": peer}, device_id_type=MESH)
        pl.semaphore_wait(sem, len(peers))


def remote(src, dst, send_sem, recv_sem, peer):
    return pltpu.make_async_remote_copy(
        src_ref=src, dst_ref=dst, send_sem=send_sem, recv_sem=recv_sem,
        device_id={"seq": peer}, device_id_type=MESH,
    )


def gather_blocks(grid, own, out, sems):
    zs, zr, ns, nr, fs, fr, ps, pr = sems
    depth = grid.depth
    started = []
    partners = []

    def slot(half, k, near, far):
        y, x = grid.place(half, near, far)
        return out.at[half, :, grid.column(-k), y, x, grid.core]

    def source(half, k, near, far):
        return own.at[half] if (k, near, far) == (0, 0, 0) else slot(half, k, near, far)

    def send(copy):
        copy.start()
        started.append(copy)
        return copy

    def to_near(half, k):
        return remote(source(half, k, 0, 0), slot(half, k, 0, 0),
                      ns.at[half, k], nr.at[half, k], grid.peer(half, 1, 0))

    def to_far(half, k, near):
        return remote(source(half, k, near, 0), slot(half, k, near, 0),
                      fs.at[half, near, k], fr.at[half, near, k], grid.peer(half, 0, 1))

    def to_partner(half, k, near, far):
        copy = remote(source(half, k, near, far), slot(half, k, near, far),
                      ps.at[half, near, far, k], pr.at[half, near, far, k], grid.partner)
        partners.append(send(copy))

    columns = {}
    for k in range(1, depth):
        for half in range(2):
            columns[half, k] = send(remote(own.at[half], slot(half, 0, 0, 0), zs.at[half, k - 1],
                                           zr.at[half, k - 1], grid.z_peer(k)))
    for half in range(2):
        out[half, :, grid.z, grid.y, grid.x, grid.core] = own[half]
    nears, fars = {}, {}
    order = [0] + [k for d in range(1, depth) for k in (d, depth - d) if d <= depth - d]
    order = list(dict.fromkeys(order))
    for i in range(depth + 1):
        for half in range(2):
            if i < depth:
                k = order[i]
                if k > 0:
                    columns[half, k].wait_recv()
                nears[half, k] = send(to_near(half, k))
                fars[half, 0, k] = send(to_far(half, k, 0))
                to_partner(half, k, 0, 0)
            if i > 0:
                k = order[i - 1]
                nears[half, k].wait_recv()
                fars[half, 1, k] = send(to_far(half, k, 1))
                to_partner(half, k, 1, 0)
    for k in order:
        for half in range(2):
            for near in range(2):
                fars[half, near, k].wait_recv()
                to_partner(half, k, near, 1)
    for copy in partners:
        copy.wait_recv()
    for copy in started:
        copy.wait_send()


def gather_sems(n):
    depth = n // 8
    dma = pltpu.SemaphoreType.DMA
    sems = []
    for shape in ((2, max(depth - 1, 1)), (2, depth), (2, 2, depth), (2, 2, 2, depth)):
        sems += [dma(shape), dma(shape)]
    return sems


def gather_kernel(n, own_ref, out_ref, *sems):
    grid = Grid(n)
    grid.barrier()
    gather_blocks(grid, own_ref, out_ref, sems)


def gather_rows(n, own):
    halves, kinds, rows, feats = own.shape
    return pl.pallas_call(
        functools.partial(gather_kernel, n),
        out_shape=jax.ShapeDtypeStruct((halves, kinds, n // 8, 2, 2, 2, rows, feats), own.dtype),
        in_specs=[pl.BlockSpec(memory_space=pltpu.VMEM)],
        out_specs=pl.BlockSpec(memory_space=pltpu.VMEM),
        scratch_shapes=gather_sems(n),
        compiler_params=pltpu.CompilerParams(
            collective_id=0, has_side_effects=True, vmem_limit_bytes=VMEM_LIMIT
        ),
        name="gather_start",
    )(own)


def reduce_kernel(n, part_ref, w_ref, out_ref, pair_in, far_out, far_in, near_out, near_in,
                  z_out, z_in, fresh, xs, xr, fs, fr, ns, nr, zs, zr, *gsems):
    grid = Grid(n)
    depth = grid.depth
    f32 = jnp.float32
    grid.barrier()
    order = list(range(1, depth)) + [0]
    started = []

    def send(copy):
        copy.start()
        started.append(copy)
        return copy

    exchange, fars, nears, columns = {}, {}, {}, {}
    for k in order:
        for half in range(2):
            col = grid.column(k)
            exchange[half, k] = send(remote(
                part_ref.at[half, :, col, :, :, 1 - grid.core], pair_in.at[half, :, k],
                xs.at[half, k], xr.at[half, k], grid.partner))

    def both(half, k, near, far):
        y, x = grid.place(half, near, far)
        return (part_ref[half, :, grid.column(k), y, x, grid.core].astype(f32)
                + pair_in[half, :, k, y, x].astype(f32))

    def far_stage(k):
        for half in range(2):
            exchange[half, k].wait_recv()
            for near in range(2):
                far_out[half, k, near] = both(half, k, near, 1).astype(far_out.dtype)
            fars[half, k] = send(remote(far_out.at[half, k], far_in.at[half, k],
                                        fs.at[half, k], fr.at[half, k], grid.peer(half, 0, 1)))

    def near_stage(k):
        for half in range(2):
            fars[half, k].wait_recv()
            near_out[half, k] = (both(half, k, 1, 0) + far_in[half, k, 1].astype(f32)
                                 ).astype(near_out.dtype)
            nears[half, k] = send(remote(near_out.at[half, k], near_in.at[half, k],
                                         ns.at[half, k], nr.at[half, k], grid.peer(half, 1, 0)))

    totals = [None, None]

    def column_stage(k):
        for half in range(2):
            nears[half, k].wait_recv()
            value = (both(half, k, 0, 0) + far_in[half, k, 0].astype(f32)
                     + near_in[half, k].astype(f32))
            if k == 0:
                totals[half] = value
            else:
                z_out[half, k - 1] = value.astype(z_out.dtype)
                columns[half, k] = send(remote(z_out.at[half, k - 1], z_in.at[half, k - 1],
                                               zs.at[half, k - 1], zr.at[half, k - 1],
                                               grid.z_peer(k)))

    for i in range(depth + 2):
        if i < depth:
            far_stage(order[i])
        if 0 < i <= depth:
            near_stage(order[i - 1])
        if i > 1:
            column_stage(order[i - 2])
    for half in range(2):
        term = totals[half]
        for k in range(1, depth):
            columns[half, k].wait_recv()
            term = term + z_in[half, k - 1].astype(f32)
        start_w = w_ref[half]
        update = start_w + term
        norm_old = jnp.sqrt(jnp.mean(start_w * start_w, axis=-1, keepdims=True) + EPS)
        norm_new = jnp.sqrt(jnp.mean(update * update, axis=-1, keepdims=True) + EPS)
        fresh[half] = (update * (norm_old / norm_new)).astype(fresh.dtype)

    gather_blocks(grid, fresh, out_ref, gsems)
    for copy in started:
        copy.wait_send()


def reduce_rows(n, part, w_own):
    halves, kinds, rows, feats = w_own.shape
    depth = n // 8
    hops = max(depth - 1, 1)
    dma = pltpu.SemaphoreType.DMA
    bf = jnp.bfloat16
    block = (kinds, rows, feats)
    return pl.pallas_call(
        functools.partial(reduce_kernel, n),
        out_shape=jax.ShapeDtypeStruct((halves, kinds, depth, 2, 2, 2, rows, feats), bf),
        in_specs=[pl.BlockSpec(memory_space=pltpu.VMEM)] * 2,
        out_specs=pl.BlockSpec(memory_space=pltpu.VMEM),
        scratch_shapes=[
            pltpu.VMEM((halves, kinds, depth, 2, 2, rows, feats), bf),
            pltpu.VMEM((halves, depth, 2) + block, bf),
            pltpu.VMEM((halves, depth, 2) + block, bf),
            pltpu.VMEM((halves, depth) + block, bf),
            pltpu.VMEM((halves, depth) + block, bf),
            pltpu.VMEM((halves, hops) + block, bf),
            pltpu.VMEM((halves, hops) + block, bf),
            pltpu.VMEM((halves,) + block, bf),
            dma((2, depth)), dma((2, depth)), dma((2, depth)), dma((2, depth)),
            dma((2, depth)), dma((2, depth)), dma((2, hops)), dma((2, hops)),
        ] + gather_sems(n),
        compiler_params=pltpu.CompilerParams(
            collective_id=1, has_side_effects=True, vmem_limit_bytes=VMEM_LIMIT
        ),
        name="reduce_gather",
    )(part, w_own)


def to_view(rows):
    tokens, groups, feats = rows.shape
    cuts = feats // LANES
    return rows.reshape(tokens, groups, cuts, LANES).transpose(0, 2, 1, 3).reshape(-1, LANES)


def from_view(view, shape):
    tokens, groups, feats = shape
    cuts = feats // LANES
    return view.reshape(tokens, cuts, groups, LANES).transpose(0, 2, 1, 3).reshape(shape)


def pick(scr, g, groups, cuts, tile):
    step = groups * cuts
    cols = [scr[pl.ds(c * groups + g, tile, stride=step), :] for c in range(cuts)]
    return jnp.concatenate(cols, axis=-1).astype(jnp.bfloat16)


def dot(a, b, dims):
    return lax.dot_general(a, b, (dims, ((), ())), preferred_element_type=jnp.float32)


def sigmoid(x):
    return 0.5 * jnp.tanh(0.5 * x) + 0.5


def terms_kernel(groups, cuts, tile, root, count_ref, k_ref, v_ref, rate_ref, b_ref, out_ref, k_scr, v_scr, acc):
    i = pl.program_id(0)

    @pl.when(i == 0)
    def _():
        acc[...] = jnp.zeros_like(acc)

    position = i * tile + lax.broadcasted_iota(jnp.int32, (tile, 1), 0)
    live = (position < count_ref[lax.axis_index("seq")]).astype(jnp.float32)
    rates = rate_ref[...].astype(jnp.float32)
    k_scr[...] = k_ref[...].astype(jnp.float32)
    v_scr[...] = v_ref[...].astype(jnp.float32)
    for g in range(groups):
        k = pick(k_scr, g, groups, cuts, tile)
        v = pick(v_scr, g, groups, cuts, tile)
        column = jnp.broadcast_to(rates[g:g + 1], (8, tile)).T[:, 0:1]
        eta = column * live / root
        err = (eta * v.astype(jnp.float32)).astype(jnp.bfloat16)
        h_one = dot(k, b_ref[g, 0], ((1,), (0,)))
        h_three = dot(k, b_ref[g, 1], ((1,), (0,)))
        back = dot(err, b_ref[g, 2], ((1,), (1,)))
        sig = sigmoid(h_one)
        gate = h_one * sig
        act = (gate * h_three).astype(jnp.bfloat16)
        d_one = (back * h_three * (sig * (1.0 + h_one * (1.0 - sig)))).astype(jnp.bfloat16)
        d_three = (back * gate).astype(jnp.bfloat16)
        acc[g, 0] += dot(k, d_one, ((0,), (0,)))
        acc[g, 1] += dot(k, d_three, ((0,), (0,)))
        acc[g, 2] += dot(act, err, ((0,), (0,)))

    @pl.when(i == pl.num_programs(0) - 1)
    def _():
        out_ref[...] = acc[...].astype(out_ref.dtype)


def local_terms(k_view, v_view, rates, counts, halves, root):
    groups, kinds, width, feats = halves.shape
    cuts = feats // LANES
    tokens = rates.shape[1]
    tile = min(512, tokens)
    rows = tile * groups * cuts
    whole = pl.BlockSpec(memory_space=pltpu.VMEM)
    return pl.pallas_call(
        functools.partial(terms_kernel, groups, cuts, tile, root),
        grid=(tokens // tile,),
        out_shape=jax.ShapeDtypeStruct(halves.shape, jnp.bfloat16),
        in_specs=[
            pl.BlockSpec(memory_space=pltpu.SMEM),
            pl.BlockSpec((rows, LANES), lambda i: (i, 0)),
            pl.BlockSpec((rows, LANES), lambda i: (i, 0)),
            pl.BlockSpec((groups, tile), lambda i: (0, i)),
            whole,
        ],
        out_specs=whole,
        scratch_shapes=[
            pltpu.VMEM((rows, LANES), jnp.float32),
            pltpu.VMEM((rows, LANES), jnp.float32),
            pltpu.VMEM(halves.shape, jnp.float32),
        ],
        compiler_params=pltpu.CompilerParams(vmem_limit_bytes=VMEM_LIMIT),
        name="local_terms",
    )(counts, k_view, v_view, rates, halves)


def apply_kernel(groups, cuts, tile, denom, count_ref, scale_ref, q_ref, c_ref, out_ref, q_scr, o_scr):
    i = pl.program_id(0)
    step = groups * cuts
    position = i * tile + lax.broadcasted_iota(jnp.int32, (tile, 1), 0)
    live = (position < count_ref[lax.axis_index("seq")]).astype(jnp.float32)
    q_scr[...] = q_ref[...].astype(jnp.float32)
    pieces = []
    total_sq = jnp.zeros((tile, 1), jnp.float32)
    for g in range(groups):
        q = pick(q_scr, g, groups, cuts, tile)
        q_one = dot(q, c_ref[g, 0], ((1,), (0,)))
        q_three = dot(q, c_ref[g, 1], ((1,), (0,)))
        a_query = (q_one * sigmoid(q_one) * q_three).astype(jnp.bfloat16)
        o = dot(a_query, c_ref[g, 2], ((1,), (0,))).astype(jnp.bfloat16)
        o = o.astype(jnp.float32) * live
        if denom is not None:
            o = o * scale_ref[g]
            total_sq = total_sq + jnp.sum(o * o, axis=-1, keepdims=True)
        pieces.append(o)
    if denom is not None:
        factor = lax.rsqrt(total_sq / denom + EPS)
        pieces = [o * factor for o in pieces]
    for g in range(groups):
        for c in range(cuts):
            o_scr[pl.ds(c * groups + g, tile, stride=step), :] = pieces[g][:, c * LANES:(c + 1) * LANES]
    out_ref[...] = o_scr[...].astype(out_ref.dtype)


def apply_rows(q_view, count, scales, fresh, tokens, denom):
    groups, kinds, width, feats = fresh.shape
    cuts = feats // LANES
    tile = min(512, tokens)
    rows = tile * groups * cuts
    smem = pl.BlockSpec(memory_space=pltpu.SMEM)
    return pl.pallas_call(
        functools.partial(apply_kernel, groups, cuts, tile, denom),
        grid=(tokens // tile,),
        out_shape=jax.ShapeDtypeStruct(q_view.shape, jnp.bfloat16),
        in_specs=[
            smem,
            smem,
            pl.BlockSpec((rows, LANES), lambda i: (i, 0)),
            pl.BlockSpec(memory_space=pltpu.VMEM),
        ],
        out_specs=pl.BlockSpec((rows, LANES), lambda i: (i, 0)),
        scratch_shapes=[
            pltpu.VMEM((rows, LANES), jnp.float32),
            pltpu.VMEM((rows, LANES), jnp.float32),
        ],
        compiler_params=pltpu.CompilerParams(vmem_limit_bytes=VMEM_LIMIT),
        name="apply_rows",
    )(count, scales, q_view, fresh)


def shards(
    queries, key_rows, value_rows, step_rates, live_counts, group_scales, w_first, w_third, w_second
):
    cap_rows, groups, feat_width = queries.shape
    seq_size = lax.axis_size("seq")
    heads = lax.axis_size("heads")
    root_total = math.sqrt(cap_rows * seq_size)
    w_own = jnp.stack([w_first, w_third, w_second], axis=1)
    full = (groups, 3, feat_width, feat_width)
    own_rows = w_own.shape[2]
    pieces = w_own.reshape(2, groups * 3 // 2, own_rows, feat_width)
    halves = gather_rows(seq_size, pieces.astype(jnp.bfloat16)).reshape(full)
    part = local_terms(
        to_view(key_rows), to_view(value_rows), step_rates, live_counts, halves, root_total
    )
    part = part.reshape(2, groups * 3 // 2, seq_size // 8, 2, 2, 2, own_rows, feat_width)
    fresh = reduce_rows(seq_size, part, pieces).reshape(full)
    denom = groups * feat_width * heads
    view = apply_rows(
        to_view(queries), live_counts, group_scales, fresh, cap_rows, denom if heads == 1 else None
    )
    fast = from_view(view, queries.shape)
    if heads == 1:
        return fast
    wide = fast.astype(jnp.float32) * group_scales[None, :, None]
    total_sq = lax.psum(jnp.sum(wide * wide, axis=(1, 2)), "heads")
    factor = lax.rsqrt(total_sq / denom + EPS)[:, None, None]
    return (wide * factor).astype(jnp.bfloat16)


def solution(mesh):
    in_specs = (
        P("seq", "heads", None),
        P("seq", "heads", None),
        P("seq", "heads", None),
        P("heads", "seq"),
        P(),
        P("heads"),
        P("heads", "seq", None),
        P("heads", "seq", None),
        P("heads", "seq", None),
    )
    out_specs = P("seq", "heads", None)
    return jax.shard_map(shards, mesh=mesh, in_specs=in_specs, out_specs=out_specs, check_vma=False)
```
